32 devices in a mesh: cp: 8 (over z, y), grp: 4 (over x, core).
Axes of the slice: x: 2, y: 2, z: 4, core: 2. Of those that a mesh axis runs over, the one named last changes fastest.
Arguments:
- queries: bfloat16 [4096, 4096], P('cp', 'grp'), parts along dimension 1, may hold values from -22.5 to 22.5
- keys: bfloat16 [4096, 512], P('cp', 'grp'), parts along dimension 1, may hold values from -7.5 to 7.5
- values: bfloat16 [4096, 512], P('cp', 'grp'), parts along dimension 1, may hold values from -6 to 6
- grad_out: bfloat16 [4096, 4096], P('cp', 'grp'), parts along dimension 1, may hold values from -6 to 6
- segments: int32 [4096], P('cp'), may hold values from 0 to 15, never falling along the last dimension, each value on 1 to 1025 neighbouring positions
Outputs:
- attended: bfloat16 [4096, 4096], P('cp', 'grp'), parts along dimension 1
- grad_queries: bfloat16 [4096, 4096], P('cp', 'grp'), parts along dimension 1
- grad_keys: bfloat16 [4096, 512], P('cp', 'grp'), parts along dimension 1
- grad_values: bfloat16 [4096, 512], P('cp', 'grp'), parts along dimension 1
The draws below stay inside these ranges and needn't reach their ends.
There are 4 independent parts, one for each index of `grp`. The reference program is written for one: setup_inputs(seed, part) draws one part's arguments, and reference() takes and returns one part's arrays. A program takes and returns all parts, laid end to end along the dimension named above; an argument that names none is the same for every part. Nothing has to cross between parts.
All inputs are finite; a program needn't handle non-finite values.
Results may differ from the reference program's by a relative error of at most 0.028.
Values may be sent and summed in bfloat16 or wider, within the bound.
A program may use at most 128 MiB of HBM per device.

```python
import math
import jax
import jax.numpy as jnp
import numpy as np
from jax import lax

HEADS = 8
HEAD_DIM = 128
TOK_DEV = 512
REACH = 2
TOKENS = 4096
DOCS = 16
DOC_MOST = 1025


def draw_keys(key, part):
    drawn = jnp.clip(jax.random.normal(jax.random.fold_in(key, 7002), (TOKENS, HEAD_DIM), jnp.float32), -4.0, 4.0)
    return drawn.astype(jnp.bfloat16)


def draw_queries(key, part):
    drawn = jnp.clip(jax.random.normal(jax.random.fold_in(key, 7003), (TOKENS, HEADS * HEAD_DIM), jnp.float32), -4.0, 4.0)
    return drawn.astype(jnp.bfloat16)


def level_of(key, dims, split, smallest, largest):
    def one(dim, blocks):
        steps = jax.random.uniform(jax.random.fold_in(jax.random.fold_in(key, 6), dim), (blocks,), jnp.float32, smallest / len(split), largest / len(split))
        return jnp.repeat(jnp.exp(steps), dims[dim] // blocks).reshape((-1,) + (1,) * (len(dims) - dim - 1))

    level = one(*split[0])
    for cut in split[1:]:
        level = level * one(*cut)
    return level


def profile(number_of, total, most, lean):
    loads = [(1 << 20) // math.isqrt(grade ** lean) + 1 for grade in range(2, number_of + 1)]
    rest, counts = total - most - (number_of - 1), [1] * (number_of - 1)
    while rest > 0:
        free = [i for i in range(number_of - 1) if counts[i] < most]
        pool, left = sum([loads[i] for i in free]), rest
        for i in free:
            more = min(most - counts[i], max(1, left * loads[i] // pool), rest)
            counts[i] = counts[i] + more
            rest = rest - more
    return np.array([most] + counts)


def ragged(stream_key, amount, total, bound, lean):
    if amount == 2:
        one = jax.random.randint(stream_key, (), max(1, total - bound), min(bound, total - 1) + 1)
        return jnp.stack([one, total - one])
    lengths = jnp.asarray(profile(amount, total, bound, lean), jnp.int32)
    twos = (amount - 1) // 2
    source_of, sink = lengths[1:1 + 2 * twos:2], lengths[2:2 + 2 * twos:2]
    room = jnp.minimum(source_of - 1, bound - sink)
    moved = jax.random.randint(jax.random.fold_in(stream_key, 1), (twos,), 0, 1 << 20) % (room + 1)
    lengths = lengths.at[1:1 + 2 * twos:2].set(source_of - moved).at[2:2 + 2 * twos:2].set(sink + moved)
    return lengths[jax.random.permutation(jax.random.fold_in(stream_key, 2), amount)]


def gaussian(own_key, extent, deviation, reach, split=(), held_as=jnp.bfloat16):
    factor_of = level_of(own_key, extent, split, -0.22, 0.18) if split else 1.0
    values = jax.random.normal(own_key, extent, jnp.float32) * deviation * factor_of
    return jnp.minimum(jnp.maximum(values, -reach), reach).astype(held_as)


def setup_inputs(seed: int = 0, part: int = 0) -> dict:
    splits = jax.random.split(jax.random.key(seed), 6)
    own_keys = jax.random.split(jax.random.fold_in(splits[5], part), 6)
    queries = draw_queries(jax.random.fold_in(jax.random.fold_in(splits[5], part), 71), part)
    keys = draw_keys(jax.random.fold_in(jax.random.fold_in(splits[5], part), 71), part)
    values = gaussian(own_keys[2], (TOKENS, HEAD_DIM), 1.0, 6.0, ((0, 8),))
    grad_out = gaussian(own_keys[3], (TOKENS, HEADS * HEAD_DIM), 1.0, 6.0, ((0, 8),))
    segments = jnp.searchsorted(jnp.cumsum(ragged(splits[4], DOCS, TOKENS, DOC_MOST, 2)), jnp.arange(TOKENS), side="right").astype(jnp.int32)
    return {"queries": queries, "keys": keys, "values": values, "grad_out": grad_out, "segments": segments}


NEG = -1e+30

def reference(queries, keys, values, grad_out, segments):
    tiles = TOKENS // TOK_DEV
    scale = 1.0 / math.sqrt(HEAD_DIM)
    pad = REACH * TOK_DEV
    span = (REACH + 1) * TOK_DEV
    keys_pad = jnp.concatenate([jnp.zeros((pad, HEAD_DIM), keys.dtype), keys], axis=0)
    values_pad = jnp.concatenate([jnp.zeros((pad, HEAD_DIM), values.dtype), values], axis=0)
    seg_pad = jnp.concatenate([jnp.full((pad,), -1, jnp.int32), segments.astype(jnp.int32)], axis=0)
    hp = lax.Precision.HIGHEST

    def per_tile(index):
        start = (index * TOK_DEV).astype(jnp.int32)
        query_tile = lax.dynamic_slice_in_dim(queries, start, TOK_DEV, 0).reshape(TOK_DEV, HEADS, HEAD_DIM).astype(jnp.float32)
        grad_tile = lax.dynamic_slice_in_dim(grad_out, start, TOK_DEV, 0).reshape(TOK_DEV, HEADS, HEAD_DIM).astype(jnp.float32)
        seg_query = lax.dynamic_slice_in_dim(segments.astype(jnp.int32), start, TOK_DEV, 0)
        key_win = lax.dynamic_slice_in_dim(keys_pad, start, span, 0).astype(jnp.float32)
        value_win = lax.dynamic_slice_in_dim(values_pad, start, span, 0).astype(jnp.float32)
        seg_win = lax.dynamic_slice_in_dim(seg_pad, start, span, 0)
        query_pos = start + jnp.arange(TOK_DEV, dtype=jnp.int32)
        key_pos = start - pad + jnp.arange(span, dtype=jnp.int32)
        allowed = (seg_query[:, None] == seg_win[None, :]) & (key_pos[None, :] <= query_pos[:, None])
        scores = jnp.einsum('qhd,kd->hqk', query_tile, key_win, precision=hp) * scale
        masked = jnp.where(allowed[None], scores, NEG)
        peak = lax.optimization_barrier(jnp.max(masked, axis=-1))
        total = lax.optimization_barrier(jnp.sum(jnp.where(allowed[None], jnp.exp(scores - peak[..., None]), 0.0), axis=-1))
        lse = peak + jnp.log(total)
        probs = jnp.where(allowed[None], jnp.exp(scores - lse[..., None]), 0.0)
        probs_low = probs.astype(jnp.bfloat16)
        attended = jnp.einsum('hqk,kd->qhd', probs_low.astype(jnp.float32), value_win, precision=hp).astype(jnp.bfloat16)
        delta = lax.optimization_barrier(jnp.sum(grad_tile * attended.astype(jnp.float32), axis=-1)).T
        dprobs = jnp.einsum('qhd,kd->hqk', grad_tile, value_win, precision=hp)
        dscores = (probs * (dprobs - delta[..., None])).astype(jnp.bfloat16).astype(jnp.float32)
        grad_q = (jnp.einsum('hqk,kd->qhd', dscores, key_win, precision=hp) * scale).astype(jnp.bfloat16)
        grad_k = jnp.einsum('hqk,qhd->kd', dscores, query_tile, precision=hp) * scale
        grad_v = jnp.einsum('hqk,qhd->kd', probs_low.astype(jnp.float32), grad_tile, precision=hp)
        return (attended.reshape(TOK_DEV, HEADS * HEAD_DIM), grad_q.reshape(TOK_DEV, HEADS * HEAD_DIM), grad_k.reshape(REACH + 1, TOK_DEV, HEAD_DIM), grad_v.reshape(REACH + 1, TOK_DEV, HEAD_DIM))
    attended, grad_q, grad_k_win, grad_v_win = lax.map(per_tile, jnp.arange(tiles, dtype=jnp.int32))
    key_total = jnp.zeros((tiles + REACH, TOK_DEV, HEAD_DIM), jnp.float32)
    value_total = jnp.zeros((tiles + REACH, TOK_DEV, HEAD_DIM), jnp.float32)
    for slot in range(REACH + 1):
        key_total = key_total.at[slot:slot + tiles].add(grad_k_win[:, slot])
        value_total = value_total.at[slot:slot + tiles].add(grad_v_win[:, slot])
    grad_keys = key_total[REACH:].reshape(TOKENS, HEAD_DIM).astype(jnp.bfloat16)
    grad_values = value_total[REACH:].reshape(TOKENS, HEAD_DIM).astype(jnp.bfloat16)
    return (attended.reshape(TOKENS, HEADS * HEAD_DIM), grad_q.reshape(TOKENS, HEADS * HEAD_DIM), grad_keys, grad_values)
```

```python
import functools
import math

import jax
import jax.numpy as jnp
from jax import lax
from jax.experimental import pallas as pl
from jax.experimental.pallas import tpu as pltpu
from jax.sharding import PartitionSpec as P

REACH = 2
NEG = -1e30
MESH = pl.DeviceIdType.MESH
NT = (((1,), (1,)), ((), ()))
F32 = jnp.float32
BF16 = jnp.bfloat16


def dot(a, b):
    return jnp.dot(a, b, preferred_element_type=F32)


def dot_nt(a, b):
    return lax.dot_general(a, b, NT, preferred_element_type=F32)


def kernel(
    n, heads, rows, size, block,
    k_ref, v_ref, seg_ref, q_hbm, g_hbm,
    o_hbm, dq_hbm, dk_ref, dv_ref,
    q_s, g_s, o_s, dq_s, kwin, vwin, segwin, ktw, vtw, kt0, vt0,
    bias0, biasw, pun, m_s, l_s, acc_s, f_s, delta_s, dqt_s,
    dkw, dvw, dk0, dv0, outbox, inbox,
    in_sem, out_sem, send_sem, recv_sem, bsend_sem, brecv_sem,
):
    me = lax.axis_index("cp")
    scale = 1.0 / math.sqrt(size)
    c2 = scale * math.log2(math.e)
    blocks = rows // block
    far = REACH * rows
    lanes = seg_ref.shape[1]
    chunks = rows // lanes

    def fetch(h):
        cols = pl.ds(pl.multiple_of(h * size, size), size)
        return (
            pltpu.make_async_copy(q_hbm.at[:, cols], q_s.at[h], in_sem.at[0, h]),
            pltpu.make_async_copy(g_hbm.at[:, cols], g_s.at[h], in_sem.at[1, h]),
        )

    def put(h):
        cols = pl.ds(pl.multiple_of(h * size, size), size)
        return (
            pltpu.make_async_copy(o_s.at[h], o_hbm.at[:, cols], out_sem.at[0, h]),
            pltpu.make_async_copy(dq_s.at[h], dq_hbm.at[:, cols], out_sem.at[1, h]),
        )

    @pl.loop(0, heads)
    def _(h):
        for copy in fetch(h):
            copy.start()

    barrier = pltpu.get_barrier_semaphore()
    steps = (-2, -1, 1, 2)

    def there(step):
        return me + step >= 0 if step < 0 else me + step < n

    for step in steps:

        @pl.when(there(step))
        def _():
            pl.semaphore_signal(barrier, inc=1, device_id={"cp": me + step}, device_id_type=MESH)

    pl.semaphore_wait(barrier, jnp.minimum(me, REACH) + jnp.minimum(n - 1 - me, REACH))

    def forward(dist):
        at = pl.ds((REACH - dist) * rows, rows)
        pairs = (
            (seg_ref, segwin.at[REACH - dist]),
            (k_ref, kwin.at[at]),
            (v_ref, vwin.at[at]),
        )
        return [
            pltpu.make_async_remote_copy(
                src_ref=src, dst_ref=dst,
                send_sem=send_sem.at[i, dist - 1], recv_sem=recv_sem.at[i, dist - 1],
                device_id={"cp": me + dist}, device_id_type=MESH,
            )
            for i, (src, dst) in enumerate(pairs)
        ]

    def back(dist):
        return [
            pltpu.make_async_remote_copy(
                src_ref=outbox.at[i, dist - 1], dst_ref=inbox.at[i, dist - 1],
                send_sem=bsend_sem.at[i, dist - 1], recv_sem=brecv_sem.at[i, dist - 1],
                device_id={"cp": me - dist}, device_id_type=MESH,
            )
            for i in range(2)
        ]

    for dist in (1, 2):

        @pl.when(there(dist))
        def _():
            for copy in forward(dist):
                copy.start()

    seg_own = seg_ref[...].astype(F32)
    line = lax.broadcasted_iota(jnp.int32, (lanes, lanes), 0)
    lane = lax.broadcasted_iota(jnp.int32, (lanes, lanes), 1)
    for kc in range(chunks):
        col = jnp.transpose(jnp.broadcast_to(seg_own[kc : kc + 1], (lanes, lanes)))
        for qc in range(chunks):
            same = col == seg_own[qc : qc + 1]
            if kc == qc:
                same = same & (line <= lane)
            value = jnp.where(same, 0.0, NEG) if kc <= qc else jnp.full((lanes, lanes), NEG, F32)
            bias0[kc * lanes : (kc + 1) * lanes, qc * lanes : (qc + 1) * lanes] = value
    kt0[...] = jnp.transpose(k_ref[...])
    vt0[...] = jnp.transpose(v_ref[...])
    dkw[...] = jnp.zeros_like(dkw)
    dvw[...] = jnp.zeros_like(dvw)
    dk0[...] = jnp.zeros_like(dk0)
    dv0[...] = jnp.zeros_like(dv0)

    @pl.loop(0, heads)
    def _(h):
        for copy in fetch(h):
            copy.wait()
        for b in range(blocks):
            qs = slice(b * block, (b + 1) * block)
            ks = slice(0, (b + 1) * block)
            s = dot_nt(k_ref[ks], q_s[h, qs]) * c2 + bias0[ks, qs]
            m = jnp.max(s, axis=0, keepdims=True)
            p = jnp.exp2(s - m)
            low = p.astype(BF16)
            pun[h, ks, qs] = low
            m_s[h, :, qs] = m
            l_s[h, :, qs] = jnp.sum(p, axis=0, keepdims=True)
            acc_s[h, :, qs] = dot(vt0[:, ks], low)

    for dist in (1, 2):
        at = slice((REACH - dist) * rows, (REACH - dist + 1) * rows)

        @pl.when(there(-dist))
        def _():
            for copy in forward(dist):
                copy.wait_recv()

        @pl.when(me - dist < 0)
        def _():
            kwin[at] = jnp.zeros((rows, size), BF16)
            vwin[at] = jnp.zeros((rows, size), BF16)
            segwin[REACH - dist] = jnp.full((chunks, lanes), -1, jnp.int32)

    for slot in range(REACH):
        seg_far = segwin[slot].astype(F32)
        at = slice(slot * rows, (slot + 1) * rows)
        for kc in range(chunks):
            col = jnp.transpose(jnp.broadcast_to(seg_far[kc : kc + 1], (lanes, lanes)))
            top = slot * rows + kc * lanes
            for qc in range(chunks):
                value = jnp.where(col == seg_own[qc : qc + 1], 0.0, NEG)
                biasw[top : top + lanes, qc * lanes : (qc + 1) * lanes] = value
        ktw[:, at] = jnp.transpose(kwin[at])
        vtw[:, at] = jnp.transpose(vwin[at])

    def far_start(b):
        return b * block

    @pl.loop(0, heads)
    def _(h):
        for b in range(blocks):
            qs = slice(b * block, (b + 1) * block)
            ks = slice(far_start(b), far)
            qb = q_s[h, qs]
            gb = g_s[h, qs]
            s = dot_nt(kwin[ks], qb) * c2 + biasw[ks, qs]
            m0 = m_s[h, :, qs]
            m = jnp.maximum(m0, jnp.max(s, axis=0, keepdims=True))
            p = jnp.exp2(s - m)
            a = jnp.exp2(m0 - m)
            inv = 1.0 / (l_s[h, :, qs] * a + jnp.sum(p, axis=0, keepdims=True))
            f0 = a * inv
            p = p * inv
            low = p.astype(BF16)
            out = (acc_s[h, :, qs] * f0 + dot(vtw[:, ks], low)).astype(BF16)
            gt = jnp.transpose(gb.astype(F32))
            outf = out.astype(F32)
            delta = jnp.sum(gt * outf, axis=0, keepdims=True)
            o_s[h, qs] = jnp.transpose(outf).astype(BF16)
            dp = dot_nt(vwin[ks], gb)
            ds = (p * (dp - delta)).astype(BF16)
            dqt_s[h, :, qs] = dot(ktw[:, ks], ds)
            dvw[ks] += dot(low, gb)
            dkw[ks] += dot(ds, qb)
            f_s[h, :, qs] = f0
            delta_s[h, :, qs] = delta
        put(h)[0].start()

    for dist in (1, 2):
        at = slice((REACH - dist) * rows, (REACH - dist + 1) * rows)
        outbox[0, dist - 1] = (dkw[at] * scale).astype(BF16)
        outbox[1, dist - 1] = dvw[at].astype(BF16)

    for dist in (1, 2):

        @pl.when(there(-dist))
        def _():
            for copy in back(dist):
                copy.start()

    @pl.loop(0, heads)
    def _(h):
        for b in range(blocks):
            qs = slice(b * block, (b + 1) * block)
            ks = slice(0, (b + 1) * block)
            qb = q_s[h, qs]
            gb = g_s[h, qs]
            p = pun[h, ks, qs].astype(F32) * f_s[h, :, qs]
            low = p.astype(BF16)
            dp = dot_nt(v_ref[ks], gb)
            ds = (p * (dp - delta_s[h, :, qs])).astype(BF16)
            dqt = dqt_s[h, :, qs] + dot(kt0[:, ks], ds)
            dq_s[h, qs] = jnp.transpose(dqt * scale).astype(BF16)
            dv0[ks] += dot(low, gb)
            dk0[ks] += dot(ds, qb)
        put(h)[1].start()

    dk0[...] = dk0[...] * scale
    for dist in (1, 2):

        @pl.when(there(dist))
        def _():
            for copy in back(dist):
                copy.wait_recv()
            dk0[...] += inbox[0, dist - 1].astype(F32)
            dv0[...] += inbox[1, dist - 1].astype(F32)

    dk_ref[...] = dk0[...].astype(BF16)
    dv_ref[...] = dv0[...].astype(BF16)

    for dist in (1, 2):

        @pl.when(there(dist))
        def _():
            for copy in forward(dist):
                copy.wait_send()

        @pl.when(there(-dist))
        def _():
            for copy in back(dist):
                copy.wait_send()

    @pl.loop(0, heads)
    def _(h):
        for copy in put(h):
            copy.wait()


def on_device(n, queries, keys, values, grad_out, segments):
    rows, width = queries.shape
    size = keys.shape[1]
    heads = width // size
    block = rows // 2
    lanes = 128
    far = REACH * rows
    vmem = pl.BlockSpec(memory_space=pltpu.VMEM)
    hbm = pl.BlockSpec(memory_space=pl.ANY)
    wide = jax.ShapeDtypeStruct((rows, width), BF16)
    thin = jax.ShapeDtypeStruct((rows, size), BF16)
    stack = pltpu.VMEM((heads, rows, size), BF16)
    row = pltpu.VMEM((heads, 1, rows), F32)
    tall = pltpu.VMEM((heads, size, rows), F32)
    dma = pltpu.SemaphoreType.DMA
    return pl.pallas_call(
        functools.partial(kernel, n, heads, rows, size, block),
        out_shape=(wide, wide, thin, thin),
        in_specs=[vmem, vmem, vmem, hbm, hbm],
        out_specs=(hbm, hbm, vmem, vmem),
        scratch_shapes=[
            stack, stack, stack, stack,
            pltpu.VMEM((far, size), BF16), pltpu.VMEM((far, size), BF16),
            pltpu.VMEM((REACH, rows // lanes, lanes), jnp.int32),
            pltpu.VMEM((size, far), BF16), pltpu.VMEM((size, far), BF16),
            pltpu.VMEM((size, rows), BF16), pltpu.VMEM((size, rows), BF16),
            pltpu.VMEM((rows, rows), F32), pltpu.VMEM((far, rows), F32),
            pltpu.VMEM((heads, rows, rows), BF16),
            row, row, tall, row, row, tall,
            pltpu.VMEM((far, size), F32), pltpu.VMEM((far, size), F32),
            pltpu.VMEM((rows, size), F32), pltpu.VMEM((rows, size), F32),
            pltpu.VMEM((2, REACH, rows, size), BF16), pltpu.VMEM((2, REACH, rows, size), BF16),
            dma((2, heads)), dma((2, heads)),
            dma((3, REACH)), dma((3, REACH)), dma((2, REACH)), dma((2, REACH)),
        ],
        compiler_params=pltpu.CompilerParams(
            collective_id=0, has_side_effects=True, vmem_limit_bytes=60 * 1024 * 1024
        ),
    )(keys, values, segments.reshape(rows // lanes, lanes), queries, grad_out)


def solution(mesh):
    placed = (P("cp", "grp"), P("cp", "grp"), P("cp", "grp"), P("cp", "grp"), P("cp"))
    return jax.shard_map(
        functools.partial(on_device, mesh.shape["cp"]),
        mesh=mesh,
        in_specs=placed,
        out_specs=(P("cp", "grp"), P("cp", "grp"), P("cp", "grp"), P("cp", "grp")),
        check_vma=False,
    )
```

```python
import functools
import math

import jax
import jax.numpy as jnp
from jax import lax
from jax.experimental import pallas as pl
from jax.experimental.pallas import tpu as pltpu
from jax.sharding import PartitionSpec as P

REACH = 2
NEG = -1e30
MESH = pl.DeviceIdType.MESH
NT = (((1,), (1,)), ((), ()))
F32 = jnp.float32
BF16 = jnp.bfloat16


def dot(a, b):
    return jnp.dot(a, b, preferred_element_type=F32)


def dot_nt(a, b):
    return lax.dot_general(a, b, NT, preferred_element_type=F32)


def kernel(
    n, heads, rows, size, block,
    k_ref, v_ref, seg_ref, q_hbm, g_hbm,
    o_hbm, dq_hbm, dk_ref, dv_ref,
    q_s, g_s, o_s, dq_s, kwin, vwin, segwin, ktw, vtw, kt0, vt0,
    bias0, biasw, pun, m_s, l_s, acc_s, f_s, delta_s, dqt_s,
    dkw, dvw, dk0, dv0, outbox, inbox, s_s, low_s, ds_s,
    in_sem, out_sem, send_sem, recv_sem, bsend_sem, brecv_sem,
):
    me = lax.axis_index("cp")
    scale = 1.0 / math.sqrt(size)
    c2 = scale * math.log2(math.e)
    blocks = rows // block
    far = REACH * rows
    cut = block // 1
    lanes = seg_ref.shape[1]
    chunks = rows // lanes

    def fetch(h):
        cols = pl.ds(pl.multiple_of(h * size, size), size)
        return (
            pltpu.make_async_copy(q_hbm.at[:, cols], q_s.at[h], in_sem.at[0, h]),
            pltpu.make_async_copy(g_hbm.at[:, cols], g_s.at[h], in_sem.at[1, h]),
        )

    def put(h):
        cols = pl.ds(pl.multiple_of(h * size, size), size)
        return (
            pltpu.make_async_copy(o_s.at[h], o_hbm.at[:, cols], out_sem.at[0, h]),
            pltpu.make_async_copy(dq_s.at[h], dq_hbm.at[:, cols], out_sem.at[1, h]),
        )

    @pl.loop(0, heads)
    def _(h):
        for copy in fetch(h):
            copy.start()

    barrier = pltpu.get_barrier_semaphore()
    steps = (-2, -1, 1, 2)

    def there(step):
        return me + step >= 0 if step < 0 else me + step < n

    for step in steps:

        @pl.when(there(step))
        def _():
            pl.semaphore_signal(barrier, inc=1, device_id={"cp": me + step}, device_id_type=MESH)

    pl.semaphore_wait(barrier, jnp.minimum(me, REACH) + jnp.minimum(n - 1 - me, REACH))

    def forward(dist):
        at = pl.ds((REACH - dist) * rows, rows)
        pairs = (
            (seg_ref, segwin.at[REACH - dist]),
            (k_ref, kwin.at[at]),
            (v_ref, vwin.at[at]),
        )
        return [
            pltpu.make_async_remote_copy(
                src_ref=src, dst_ref=dst,
                send_sem=send_sem.at[i, dist - 1], recv_sem=recv_sem.at[i, dist - 1],
                device_id={"cp": me + dist}, device_id_type=MESH,
            )
            for i, (src, dst) in enumerate(pairs)
        ]

    def back(dist):
        return [
            pltpu.make_async_remote_copy(
                src_ref=outbox.at[i, dist - 1], dst_ref=inbox.at[i, dist - 1],
                send_sem=bsend_sem.at[i, dist - 1], recv_sem=brecv_sem.at[i, dist - 1],
                device_id={"cp": me - dist}, device_id_type=MESH,
            )
            for i in range(2)
        ]

    for dist in (1, 2):

        @pl.when(there(dist))
        def _():
            for copy in forward(dist):
                copy.start()

    seg_own = seg_ref[...].astype(F32)
    line = lax.broadcasted_iota(jnp.int32, (lanes, lanes), 0)
    lane = lax.broadcasted_iota(jnp.int32, (lanes, lanes), 1)
    for kc in range(chunks):
        col = jnp.transpose(jnp.broadcast_to(seg_own[kc : kc + 1], (lanes, lanes)))
        for qc in range(chunks):
            same = col == seg_own[qc : qc + 1]
            if kc == qc:
                same = same & (line <= lane)
            value = jnp.where(same, 0.0, NEG) if kc <= qc else jnp.full((lanes, lanes), NEG, F32)
            bias0[kc * lanes : (kc + 1) * lanes, qc * lanes : (qc + 1) * lanes] = value
    kt0[...] = jnp.transpose(k_ref[...])
    vt0[...] = jnp.transpose(v_ref[...])
    dkw[...] = jnp.zeros_like(dkw)
    dvw[...] = jnp.zeros_like(dvw)
    dk0[...] = jnp.zeros_like(dk0)
    dv0[...] = jnp.zeros_like(dv0)

    def local_chunks():
        return [(k, k + cut, k // block * block, rows) for k in range(0, rows, cut)]

    def far_chunks():
        return [(k, k + cut, 0, min(rows, (k // block + 1) * block)) for k in range(0, far, cut)]

    def eights(x):
        return x.reshape(x.shape[0] // 8, 8, x.shape[1])

    def scores(h, chunks_of, keys, bias, tops):
        for k0, k1, q0, q1 in chunks_of:
            s = dot_nt(keys[k0:k1], q_s[h, q0:q1]) * c2 + bias[k0:k1, q0:q1]
            s_s[k0:k1, q0:q1] = s
            top = jnp.max(eights(s), axis=0)
            for b in range(q0 // block, q1 // block):
                part = top[:, b * block - q0 : (b + 1) * block - q0]
                tops[b] = part if tops[b] is None else jnp.maximum(tops[b], part)
        return jnp.concatenate([jnp.max(t, axis=0, keepdims=True) for t in tops], axis=1)

    def weights(chunks_of, m, store):
        sums = [None] * blocks
        for k0, k1, q0, q1 in chunks_of:
            p = jnp.exp2(s_s[k0:k1, q0:q1] - m[:, q0:q1])
            store[k0:k1, q0:q1] = p.astype(BF16)
            part = jnp.sum(eights(p), axis=0)
            for b in range(q0 // block, q1 // block):
                one = part[:, b * block - q0 : (b + 1) * block - q0]
                sums[b] = one if sums[b] is None else sums[b] + one
        return jnp.concatenate([jnp.sum(t, axis=0, keepdims=True) for t in sums], axis=1)

    def back_chunks(h, chunks_of, low_of, factor, delta, values, dk_sum, dv_sum):
        for k0, k1, q0, q1 in chunks_of:
            p = low_of[k0:k1, q0:q1].astype(F32) * factor[:, q0:q1]
            dp = dot_nt(values[k0:k1], g_s[h, q0:q1])
            ds = (p * (dp - delta[:, q0:q1])).astype(BF16)
            ds_s[k0:k1, q0:q1] = ds
            dv_sum[k0:k1] += dot(p.astype(BF16), g_s[h, q0:q1])
            dk_sum[k0:k1] += dot(ds, q_s[h, q0:q1])

    def local_dot(left, right):
        return [dot(left[:, : (b + 1) * block], right[: (b + 1) * block, b * block : (b + 1) * block]) for b in range(blocks)]

    def far_dot(left, right):
        return [dot(left[:, b * block :], right[b * block :, b * block : (b + 1) * block]) for b in range(blocks)]

    @pl.loop(0, heads)
    def _(h):
        for copy in fetch(h):
            copy.wait()
        m = scores(h, local_chunks(), k_ref, bias0, [None] * blocks)
        m_s[h] = m
        l_s[h] = weights(local_chunks(), m, pun.at[h])
        for b, part in enumerate(local_dot(vt0, pun.at[h])):
            acc_s[h, :, b * block : (b + 1) * block] = part

    for dist in (1, 2):
        at = slice((REACH - dist) * rows, (REACH - dist + 1) * rows)

        @pl.when(there(-dist))
        def _():
            for copy in forward(dist):
                copy.wait_recv()

        @pl.when(me - dist < 0)
        def _():
            kwin[at] = jnp.zeros((rows, size), BF16)
            vwin[at] = jnp.zeros((rows, size), BF16)
            segwin[REACH - dist] = jnp.full((chunks, lanes), -1, jnp.int32)

    for slot in range(REACH):
        seg_far = segwin[slot].astype(F32)
        at = slice(slot * rows, (slot + 1) * rows)
        for kc in range(chunks):
            col = jnp.transpose(jnp.broadcast_to(seg_far[kc : kc + 1], (lanes, lanes)))
            top = slot * rows + kc * lanes
            for qc in range(chunks):
                value = jnp.where(col == seg_own[qc : qc + 1], 0.0, NEG)
                biasw[top : top + lanes, qc * lanes : (qc + 1) * lanes] = value
        ktw[:, at] = jnp.transpose(kwin[at])
        vtw[:, at] = jnp.transpose(vwin[at])

    @pl.loop(0, heads)
    def _(h):
        m0 = m_s[h]
        m = jnp.maximum(m0, scores(h, far_chunks(), kwin, biasw, [None] * blocks))
        a = jnp.exp2(m0 - m)
        inv = 1.0 / (l_s[h] * a + weights(far_chunks(), m, low_s))
        f0 = a * inv
        f_s[h] = f0
        deltas = []
        for b, part in enumerate(far_dot(vtw, low_s)):
            qs = slice(b * block, (b + 1) * block)
            out = (acc_s[h, :, qs] * f0[:, qs] + part * inv[:, qs]).astype(BF16).astype(F32)
            gt = jnp.transpose(g_s[h, qs].astype(F32))
            deltas.append(jnp.sum(gt * out, axis=0, keepdims=True))
            o_s[h, qs] = jnp.transpose(out).astype(BF16)
        delta = jnp.concatenate(deltas, axis=1)
        delta_s[h] = delta
        back_chunks(h, far_chunks(), low_s, inv, delta, vwin, dkw, dvw)
        for b, part in enumerate(far_dot(ktw, ds_s)):
            dqt_s[h, :, b * block : (b + 1) * block] = part
        put(h)[0].start()

    for dist in (1, 2):
        at = slice((REACH - dist) * rows, (REACH - dist + 1) * rows)
        outbox[0, dist - 1] = (dkw[at] * scale).astype(BF16)
        outbox[1, dist - 1] = dvw[at].astype(BF16)

    for dist in (1, 2):

        @pl.when(there(-dist))
        def _():
            for copy in back(dist):
                copy.start()

    @pl.loop(0, heads)
    def _(h):
        back_chunks(h, local_chunks(), pun.at[h], f_s[h], delta_s[h], v_ref, dk0, dv0)
        for b, part in enumerate(local_dot(kt0, ds_s)):
            qs = slice(b * block, (b + 1) * block)
            dq_s[h, qs] = jnp.transpose((dqt_s[h, :, qs] + part) * scale).astype(BF16)
        put(h)[1].start()

    dk0[...] = dk0[...] * scale
    for dist in (1, 2):

        @pl.when(there(dist))
        def _():
            for copy in back(dist):
                copy.wait_recv()
            dk0[...] += inbox[0, dist - 1].astype(F32)
            dv0[...] += inbox[1, dist - 1].astype(F32)

    dk_ref[...] = dk0[...].astype(BF16)
    dv_ref[...] = dv0[...].astype(BF16)

    for dist in (1, 2):

        @pl.when(there(dist))
        def _():
            for copy in forward(dist):
                copy.wait_send()

        @pl.when(there(-dist))
        def _():
            for copy in back(dist):
                copy.wait_send()

    @pl.loop(0, heads)
    def _(h):
        for copy in put(h):
            copy.wait()


def on_device(n, queries, keys, values, grad_out, segments):
    rows, width = queries.shape
    size = keys.shape[1]
    heads = width // size
    block = rows // 2
    lanes = 128
    far = REACH * rows
    vmem = pl.BlockSpec(memory_space=pltpu.VMEM)
    hbm = pl.BlockSpec(memory_space=pl.ANY)
    wide = jax.ShapeDtypeStruct((rows, width), BF16)
    thin = jax.ShapeDtypeStruct((rows, size), BF16)
    stack = pltpu.VMEM((heads, rows, size), BF16)
    row = pltpu.VMEM((heads, 1, rows), F32)
    tall = pltpu.VMEM((heads, size, rows), F32)
    dma = pltpu.SemaphoreType.DMA
    return pl.pallas_call(
        functools.partial(kernel, n, heads, rows, size, block),
        out_shape=(wide, wide, thin, thin),
        in_specs=[vmem, vmem, vmem, hbm, hbm],
        out_specs=(hbm, hbm, vmem, vmem),
        scratch_shapes=[
            stack, stack, stack, stack,
            pltpu.VMEM((far, size), BF16), pltpu.VMEM((far, size), BF16),
            pltpu.VMEM((REACH, rows // lanes, lanes), jnp.int32),
            pltpu.VMEM((size, far), BF16), pltpu.VMEM((size, far), BF16),
            pltpu.VMEM((size, rows), BF16), pltpu.VMEM((size, rows), BF16),
            pltpu.VMEM((rows, rows), F32), pltpu.VMEM((far, rows), F32),
            pltpu.VMEM((heads, rows, rows), BF16),
            row, row, tall, row, row, tall,
            pltpu.VMEM((far, size), F32), pltpu.VMEM((far, size), F32),
            pltpu.VMEM((rows, size), F32), pltpu.VMEM((rows, size), F32),
            pltpu.VMEM((2, REACH, rows, size), BF16), pltpu.VMEM((2, REACH, rows, size), BF16),
            pltpu.VMEM((far, rows), F32), pltpu.VMEM((far, rows), BF16), pltpu.VMEM((far, rows), BF16),
            dma((2, heads)), dma((2, heads)),
            dma((3, REACH)), dma((3, REACH)), dma((2, REACH)), dma((2, REACH)),
        ],
        compiler_params=pltpu.CompilerParams(
            collective_id=0, has_side_effects=True, vmem_limit_bytes=60 * 1024 * 1024
        ),
    )(keys, values, segments.reshape(rows // lanes, lanes), queries, grad_out)


def solution(mesh):
    placed = (P("cp", "grp"), P("cp", "grp"), P("cp", "grp"), P("cp", "grp"), P("cp"))
    return jax.shard_map(
        functools.partial(on_device, mesh.shape["cp"]),
        mesh=mesh,
        in_specs=placed,
        out_specs=(P("cp", "grp"), P("cp", "grp"), P("cp", "grp"), P("cp", "grp")),
        check_vma=False,
    )
```

```python
import functools
import math

import jax
import jax.numpy as jnp
from jax import lax
from jax.experimental import pallas as pl
from jax.experimental.pallas import tpu as pltpu
from jax.sharding import PartitionSpec as P

REACH = 2
NEG = -1e30
MESH = pl.DeviceIdType.MESH
NT = (((1,), (1,)), ((), ()))
F32 = jnp.float32
BF16 = jnp.bfloat16


VMEM_MIB = 48
FWD = 2
BWD = 2


def dist_before(dist):
    return 0 if dist == REACH else REACH


def dot(a, b):
    return jnp.dot(a, b, preferred_element_type=F32)


def dot_nt(a, b):
    return lax.dot_general(a, b, NT, preferred_element_type=F32)


def kernel(
    n, heads, rows, size, block,
    k_ref, v_ref, seg_ref, q_hbm, g_hbm,
    o_hbm, dq_hbm, dk_ref, dv_ref,
    q_s, g_s, o_s, dq_s, kwin, vwin, segwin, ktw, vtw, kt0, vt0,
    bias0, biasw, pun, m_s, l_s, acc_s, f_s, delta_s, dqt_s,
    dkw, dvw, dk0, dv0, outbox, inbox, s_s, ds_s,
    in_sem, out_sem, send_sem, recv_sem, relay_sem, bsend_sem, brecv_sem,
):
    me = lax.axis_index("cp")
    scale = 1.0 / math.sqrt(size)
    c2 = scale * math.log2(math.e)
    blocks = rows // block
    far = REACH * rows
    cut = block // 1
    lanes = seg_ref.shape[1]
    chunks = rows // lanes

    def fetch(h):
        cols = pl.ds(pl.multiple_of(h * size, size), size)
        return (
            pltpu.make_async_copy(q_hbm.at[:, cols], q_s.at[h], in_sem.at[0, h]),
            pltpu.make_async_copy(g_hbm.at[:, cols], g_s.at[h], in_sem.at[1, h]),
        )

    def put(h):
        cols = pl.ds(pl.multiple_of(h * size, size), size)
        return (
            pltpu.make_async_copy(o_s.at[h], o_hbm.at[:, cols], out_sem.at[0, h]),
            pltpu.make_async_copy(dq_s.at[h], dq_hbm.at[:, cols], out_sem.at[1, h]),
        )

    @pl.loop(0, heads)
    def _(h):
        for copy in fetch(h):
            copy.start()

    barrier = pltpu.get_barrier_semaphore()
    steps = (-2, -1, 1, 2)

    def there(step):
        return me + step >= 0 if step < 0 else me + step < n

    for step in steps:

        @pl.when(there(step))
        def _():
            pl.semaphore_signal(barrier, inc=1, device_id={"cp": me + step}, device_id_type=MESH)

    pl.semaphore_wait(barrier, jnp.minimum(me, REACH) + jnp.minimum(n - 1 - me, REACH))

    def forward(dist):
        at = pl.ds((REACH - dist) * rows, rows)
        pairs = (
            (seg_ref, segwin.at[REACH - dist]),
            (k_ref, kwin.at[at]),
            (v_ref, vwin.at[at]),
        )
        return [
            pltpu.make_async_remote_copy(
                src_ref=src, dst_ref=dst,
                send_sem=send_sem.at[i, dist - 1], recv_sem=recv_sem.at[i, dist - 1],
                device_id={"cp": me + dist}, device_id_type=MESH,
            )
            for i, (src, dst) in enumerate(pairs)
        ]

    def relay(i):
        held = (kwin, vwin)[i]
        return pltpu.make_async_remote_copy(
            src_ref=held.at[pl.ds(0, rows)], dst_ref=held.at[pl.ds(rows, rows)],
            send_sem=relay_sem.at[i], recv_sem=recv_sem.at[i + 1, 0],
            device_id={"cp": me - 1}, device_id_type=MESH,
        )

    odd = lax.rem(me, 2) == 1
    relays = odd & (me >= REACH)
    direct = (me + 1 < n) & ((lax.rem(me, 2) == 0) | (me + REACH >= n))

    def back(dist):
        return [
            pltpu.make_async_remote_copy(
                src_ref=outbox.at[i, dist - 1], dst_ref=inbox.at[i, dist - 1],
                send_sem=bsend_sem.at[i, dist - 1], recv_sem=brecv_sem.at[i, dist - 1],
                device_id={"cp": me - dist}, device_id_type=MESH,
            )
            for i in range(2)
        ]

    for dist in (2, 1):

        @pl.when(there(dist))
        def _():
            forward(dist)[0].start()

    @pl.when(there(2))
    def _():
        for copy in forward(2)[1:]:
            copy.start()

    @pl.when(direct)
    def _():
        for copy in forward(1)[1:]:
            copy.start()

    seg_own = seg_ref[...].astype(F32)
    line = lax.broadcasted_iota(jnp.int32, (lanes, lanes), 0)
    lane = lax.broadcasted_iota(jnp.int32, (lanes, lanes), 1)
    for kc in range(chunks):
        col = jnp.transpose(jnp.broadcast_to(seg_own[kc : kc + 1], (lanes, lanes)))
        for qc in range(chunks):
            same = col == seg_own[qc : qc + 1]
            if kc == qc:
                same = same & (line <= lane)
            value = jnp.where(same, 0.0, NEG) if kc <= qc else jnp.full((lanes, lanes), NEG, F32)
            bias0[kc * lanes : (kc + 1) * lanes, qc * lanes : (qc + 1) * lanes] = value
    kt0[...] = jnp.transpose(k_ref[...])
    vt0[...] = jnp.transpose(v_ref[...])
    dkw[...] = jnp.zeros_like(dkw)
    dvw[...] = jnp.zeros_like(dvw)
    dk0[...] = jnp.zeros_like(dk0)
    dv0[...] = jnp.zeros_like(dv0)

    def local_chunks():
        return [(k, k + cut, k // block * block, rows) for k in range(0, rows, cut)]

    def far_chunks(dist):
        ends = [min(rows, (k // block + 1) * block) if dist == REACH else rows for k in range(0, rows, cut)]
        return [(k, k + cut, 0, end) for k, end in zip(range(0, rows, cut), ends)]

    def eights(x):
        return x.reshape(x.shape[0] // 8, 8, x.shape[1])

    def scores(h, chunks_of, keys, bias, tops):
        for k0, k1, q0, q1 in chunks_of:
            s = dot_nt(keys[k0:k1], q_s[h, q0:q1]) * c2 + bias[k0:k1, q0:q1]
            s_s[k0:k1, q0:q1] = s
            top = jnp.max(eights(s), axis=0)
            for b in range(q0 // block, q1 // block):
                part = top[:, b * block - q0 : (b + 1) * block - q0]
                tops[b] = part if tops[b] is None else jnp.maximum(tops[b], part)
        return jnp.concatenate([jnp.max(t, axis=0, keepdims=True) for t in tops], axis=1)

    def weights(chunks_of, m, store):
        sums = [None] * blocks
        for k0, k1, q0, q1 in chunks_of:
            p = jnp.exp2(s_s[k0:k1, q0:q1] - m[:, q0:q1])
            store[k0:k1, q0:q1] = p.astype(BF16)
            part = jnp.sum(eights(p), axis=0)
            for b in range(q0 // block, q1 // block):
                one = part[:, b * block - q0 : (b + 1) * block - q0]
                sums[b] = one if sums[b] is None else sums[b] + one
        return jnp.concatenate([jnp.sum(t, axis=0, keepdims=True) for t in sums], axis=1)

    def back_chunks(h, chunks_of, low_of, factor, delta, values, dk_sum, dv_sum):
        for k0, k1, q0, q1 in chunks_of:
            p = low_of[k0:k1, q0:q1].astype(F32) * factor[:, q0:q1]
            dp = dot_nt(values[k0:k1], g_s[h, q0:q1])
            ds = (p * (dp - delta[:, q0:q1])).astype(BF16)
            ds_s[k0:k1, q0:q1] = ds
            dv_sum[k0:k1] += dot(p.astype(BF16), g_s[h, q0:q1])
            dk_sum[k0:k1] += dot(ds, q_s[h, q0:q1])

    def local_dot(left, right):
        return [dot(left[:, : (b + 1) * block], right[: (b + 1) * block, b * block : (b + 1) * block]) for b in range(blocks)]

    def far_dot(dist, left, right):
        first = block if dist == REACH else 0
        return [dot(left[:, b * first :], right[b * first :, b * block : (b + 1) * block]) for b in range(blocks)]

    def slot_of(dist):
        return pl.ds((REACH - dist) * rows, rows)

    @pl.loop(0, heads)
    def _(h):
        for copy in fetch(h):
            copy.wait()
        m = scores(h, local_chunks(), k_ref, bias0, [None] * blocks)
        m_s[0, h] = m
        l_s[h] = weights(local_chunks(), m, pun.at[0, h])
        for b, part in enumerate(local_dot(vt0, pun.at[0, h])):
            acc_s[h, :, b * block : (b + 1) * block] = part

    for dist in (2, 1):

        @pl.when(there(-dist))
        def _():
            forward(dist)[0].wait_recv()

        @pl.when(me - dist < 0)
        def _():
            kwin[slot_of(dist)] = jnp.zeros((rows, size), BF16)
            vwin[slot_of(dist)] = jnp.zeros((rows, size), BF16)
            segwin[REACH - dist] = jnp.full((chunks, lanes), -1, jnp.int32)

        seg_far = segwin[REACH - dist].astype(F32)
        for kc in range(chunks):
            col = jnp.transpose(jnp.broadcast_to(seg_far[kc : kc + 1], (lanes, lanes)))
            top = (REACH - dist) * rows + kc * lanes
            for qc in range(chunks):
                value = jnp.where(col == seg_own[qc : qc + 1], 0.0, NEG)
                biasw[top : top + lanes, qc * lanes : (qc + 1) * lanes] = value

    @pl.when(there(-2))
    def _():
        forward(2)[1].wait_recv()

    @pl.when(relays)
    def _():
        relay(0).start()

    @pl.when(there(-2))
    def _():
        forward(2)[2].wait_recv()

    @pl.when(relays)
    def _():
        relay(1).start()

    for dist in (2, 1):
        at = slot_of(dist)
        if dist == 1:

            @pl.when(there(-1))
            def _():
                for copy in forward(1)[1:]:
                    copy.wait_recv()

        ktw[:, at] = jnp.transpose(kwin[at])
        vtw[:, at] = jnp.transpose(vwin[at])

        @pl.loop(0, heads, unroll=FWD)
        def _(h):
            m0 = m_s[dist_before(dist), h]
            m = jnp.maximum(m0, scores(h, far_chunks(dist), kwin.at[at], biasw.at[at], [None] * blocks))
            m_s[dist, h] = m
            a = jnp.exp2(m0 - m)
            total = l_s[h] * a + weights(far_chunks(dist), m, pun.at[dist, h])
            parts = far_dot(dist, vtw.at[:, at], pun.at[dist, h])
            sums = []
            for b, part in enumerate(parts):
                qs = slice(b * block, (b + 1) * block)
                sums.append(acc_s[h, :, qs] * a[:, qs] + part)
            if dist == REACH:
                l_s[h] = total
                for b in range(blocks):
                    acc_s[h, :, b * block : (b + 1) * block] = sums[b]
            else:
                inv = 1.0 / total
                f_s[1, h] = inv
                f_s[2, h] = a * inv
                f_s[0, h] = jnp.exp2(m_s[0, h] - m) * inv
                for b in range(blocks):
                    qs = slice(b * block, (b + 1) * block)
                    out = (sums[b] * inv[:, qs]).astype(BF16).astype(F32)
                    gt = jnp.transpose(g_s[h, qs].astype(F32))
                    delta_s[h, :, qs] = jnp.sum(gt * out, axis=0, keepdims=True)
                    o_s[h, qs] = jnp.transpose(out).astype(BF16)
                put(h)[0].start()

    for dist in (2, 1):
        at = slot_of(dist)

        @pl.loop(0, heads, unroll=BWD)
        def _(h):
            back_chunks(h, far_chunks(dist), pun.at[dist, h], f_s[dist, h], delta_s[h], vwin.at[at], dkw.at[at], dvw.at[at])
            for b, part in enumerate(far_dot(dist, ktw.at[:, at], ds_s)):
                qs = slice(b * block, (b + 1) * block)
                dqt_s[h, :, qs] = part if dist == REACH else dqt_s[h, :, qs] + part

        outbox[0, dist - 1] = (dkw[at] * scale).astype(BF16)
        outbox[1, dist - 1] = dvw[at].astype(BF16)

        @pl.when(there(-dist))
        def _():
            for copy in back(dist):
                copy.start()

    @pl.loop(0, heads, unroll=BWD)
    def _(h):
        back_chunks(h, local_chunks(), pun.at[0, h], f_s[0, h], delta_s[h], v_ref, dk0, dv0)
        for b, part in enumerate(local_dot(kt0, ds_s)):
            qs = slice(b * block, (b + 1) * block)
            dq_s[h, qs] = jnp.transpose((dqt_s[h, :, qs] + part) * scale).astype(BF16)
        put(h)[1].start()

    dk0[...] = dk0[...] * scale
    for dist in (2, 1):

        @pl.when(there(dist))
        def _():
            for copy in back(dist):
                copy.wait_recv()
            dk0[...] += inbox[0, dist - 1].astype(F32)
            dv0[...] += inbox[1, dist - 1].astype(F32)

    dk_ref[...] = dk0[...].astype(BF16)
    dv_ref[...] = dv0[...].astype(BF16)

    for dist in (1, 2):

        @pl.when(there(dist))
        def _():
            forward(dist)[0].wait_send()

        @pl.when(direct if dist == 1 else there(dist))
        def _():
            for copy in forward(dist)[1:]:
                copy.wait_send()

        @pl.when(there(-dist))
        def _():
            for copy in back(dist):
                copy.wait_send()

    @pl.when(relays)
    def _():
        for i in range(2):
            relay(i).wait_send()

    @pl.loop(0, heads)
    def _(h):
        for copy in put(h):
            copy.wait()


def on_device(n, queries, keys, values, grad_out, segments):
    rows, width = queries.shape
    size = keys.shape[1]
    heads = width // size
    block = rows // 2
    lanes = 128
    far = REACH * rows
    vmem = pl.BlockSpec(memory_space=pltpu.VMEM)
    hbm = pl.BlockSpec(memory_space=pl.ANY)
    far_in = pl.BlockSpec(memory_space=pltpu.HBM)
    wide = jax.ShapeDtypeStruct((rows, width), BF16)
    thin = jax.ShapeDtypeStruct((rows, size), BF16)
    stack = pltpu.VMEM((heads, rows, size), BF16)
    row = pltpu.VMEM((heads, 1, rows), F32)
    rows3 = pltpu.VMEM((REACH + 1, heads, 1, rows), F32)
    tall = pltpu.VMEM((heads, size, rows), F32)
    dma = pltpu.SemaphoreType.DMA
    return pl.pallas_call(
        functools.partial(kernel, n, heads, rows, size, block),
        out_shape=(wide, wide, thin, thin),
        in_specs=[vmem, vmem, vmem, far_in, far_in],
        out_specs=(hbm, hbm, vmem, vmem),
        scratch_shapes=[
            stack, stack, stack, stack,
            pltpu.VMEM((far, size), BF16), pltpu.VMEM((far, size), BF16),
            pltpu.VMEM((REACH, rows // lanes, lanes), jnp.int32),
            pltpu.VMEM((size, far), BF16), pltpu.VMEM((size, far), BF16),
            pltpu.VMEM((size, rows), BF16), pltpu.VMEM((size, rows), BF16),
            pltpu.VMEM((rows, rows), F32), pltpu.VMEM((far, rows), F32),
            pltpu.VMEM((REACH + 1, heads, rows, rows), BF16),
            rows3, row, tall, rows3, row, tall,
            pltpu.VMEM((far, size), F32), pltpu.VMEM((far, size), F32),
            pltpu.VMEM((rows, size), F32), pltpu.VMEM((rows, size), F32),
            pltpu.VMEM((2, REACH, rows, size), BF16), pltpu.VMEM((2, REACH, rows, size), BF16),
            pltpu.VMEM((rows, rows), F32), pltpu.VMEM((rows, rows), BF16),
            dma((2, heads)), dma((2, heads)),
            dma((3, REACH)), dma((3, REACH)), dma((2,)), dma((2, REACH)), dma((2, REACH)),
        ],
        compiler_params=pltpu.CompilerParams(
            collective_id=0, has_side_effects=True,
            vmem_limit_bytes=VMEM_MIB * 1024 * 1024,
        ),
    )(keys, values, segments.reshape(rows // lanes, lanes), queries, grad_out)


def solution(mesh):
    placed = (P("cp", "grp"), P("cp", "grp"), P("cp", "grp"), P("cp", "grp"), P("cp"))
    return jax.shard_map(
        functools.partial(on_device, mesh.shape["cp"]),
        mesh=mesh,
        in_specs=placed,
        out_specs=(P("cp", "grp"), P("cp", "grp"), P("cp", "grp"), P("cp", "grp")),
        check_vma=False,
    )
```

```python
import functools
import math

import jax
import jax.numpy as jnp
from jax import lax
from jax.experimental import pallas as pl
from jax.experimental.pallas import tpu as pltpu
from jax.sharding import PartitionSpec as P

REACH = 2
NEG = -1e30
MESH = pl.DeviceIdType.MESH
NT = (((1,), (1,)), ((), ()))
F32 = jnp.float32
BF16 = jnp.bfloat16


VMEM_MIB = 60
GROUP = 2


def dist_before(dist):
    return 0 if dist == REACH else REACH


def dot(a, b):
    return jnp.dot(a, b, preferred_element_type=F32)


def dot_nt(a, b):
    return lax.dot_general(a, b, NT, preferred_element_type=F32)


def kernel(
    n, heads, rows, size, block,
    k_ref, v_ref, seg_ref, q_hbm, g_hbm,
    o_hbm, dq_hbm, dk_ref, dv_ref,
    q_s, g_s, o_s, dq_s, kwin, vwin, segwin, ktw, vtw, kt0, vt0,
    bias0, biasw, pun, m_s, l_s, acc_s, f_s, delta_s, dqt_s,
    dkw, dvw, dk0, dv0, outbox, inbox, s_s, low_s, ds_s,
    in_sem, out_sem, send_sem, recv_sem, relay_sem, bsend_sem, brecv_sem,
):
    me = lax.axis_index("cp")
    scale = 1.0 / math.sqrt(size)
    c2 = scale * math.log2(math.e)
    blocks = rows // block
    far = REACH * rows
    cut = block // 1
    lanes = seg_ref.shape[1]
    chunks = rows // lanes

    def fetch(h):
        cols = pl.ds(pl.multiple_of(h * size, size), size)
        return (
            pltpu.make_async_copy(q_hbm.at[:, cols], q_s.at[h], in_sem.at[0, h]),
            pltpu.make_async_copy(g_hbm.at[:, cols], g_s.at[h], in_sem.at[1, h]),
        )

    def put(h):
        cols = pl.ds(pl.multiple_of(h * size, size), size)
        return (
            pltpu.make_async_copy(o_s.at[h], o_hbm.at[:, cols], out_sem.at[0, h]),
            pltpu.make_async_copy(dq_s.at[h], dq_hbm.at[:, cols], out_sem.at[1, h]),
        )

    @pl.loop(0, heads)
    def _(h):
        for copy in fetch(h):
            copy.start()

    barrier = pltpu.get_barrier_semaphore()
    steps = (-2, -1, 1, 2)

    def there(step):
        return me + step >= 0 if step < 0 else me + step < n

    for step in steps:

        @pl.when(there(step))
        def _():
            pl.semaphore_signal(barrier, inc=1, device_id={"cp": me + step}, device_id_type=MESH)

    pl.semaphore_wait(barrier, jnp.minimum(me, REACH) + jnp.minimum(n - 1 - me, REACH))

    def forward(dist):
        at = pl.ds((REACH - dist) * rows, rows)
        pairs = (
            (seg_ref, segwin.at[REACH - dist]),
            (k_ref, kwin.at[at]),
            (v_ref, vwin.at[at]),
        )
        return [
            pltpu.make_async_remote_copy(
                src_ref=src, dst_ref=dst,
                send_sem=send_sem.at[i, dist - 1], recv_sem=recv_sem.at[i, dist - 1],
                device_id={"cp": me + dist}, device_id_type=MESH,
            )
            for i, (src, dst) in enumerate(pairs)
        ]

    def relay(i):
        held = (kwin, vwin)[i]
        return pltpu.make_async_remote_copy(
            src_ref=held.at[pl.ds(0, rows)], dst_ref=held.at[pl.ds(rows, rows)],
            send_sem=relay_sem.at[i], recv_sem=recv_sem.at[i + 1, 0],
            device_id={"cp": me - 1}, device_id_type=MESH,
        )

    odd = lax.rem(me, 2) == 1
    relays = odd & (me >= REACH)
    direct = (me + 1 < n) & ((lax.rem(me, 2) == 0) | (me + REACH >= n))

    def back(dist):
        return [
            pltpu.make_async_remote_copy(
                src_ref=outbox.at[i, dist - 1], dst_ref=inbox.at[i, dist - 1],
                send_sem=bsend_sem.at[i, dist - 1], recv_sem=brecv_sem.at[i, dist - 1],
                device_id={"cp": me - dist}, device_id_type=MESH,
            )
            for i in range(2)
        ]

    for dist in (2, 1):

        @pl.when(there(dist))
        def _():
            forward(dist)[0].start()

    @pl.when(there(2))
    def _():
        for copy in forward(2)[1:]:
            copy.start()

    @pl.when(direct)
    def _():
        for copy in forward(1)[1:]:
            copy.start()

    seg_own = seg_ref[...].astype(F32)
    line = lax.broadcasted_iota(jnp.int32, (lanes, lanes), 0)
    lane = lax.broadcasted_iota(jnp.int32, (lanes, lanes), 1)
    for kc in range(chunks):
        col = jnp.transpose(jnp.broadcast_to(seg_own[kc : kc + 1], (lanes, lanes)))
        for qc in range(chunks):
            same = col == seg_own[qc : qc + 1]
            if kc == qc:
                same = same & (line <= lane)
            value = jnp.where(same, 0.0, NEG) if kc <= qc else jnp.full((lanes, lanes), NEG, F32)
            bias0[kc * lanes : (kc + 1) * lanes, qc * lanes : (qc + 1) * lanes] = value
    kt0[...] = jnp.transpose(k_ref[...])
    vt0[...] = jnp.transpose(v_ref[...])
    dkw[...] = jnp.zeros_like(dkw)
    dvw[...] = jnp.zeros_like(dvw)
    dk0[...] = jnp.zeros_like(dk0)
    dv0[...] = jnp.zeros_like(dv0)

    def local_chunks():
        return [(k, k + cut, k // block * block, rows) for k in range(0, rows, cut)]

    def far_chunks(dist):
        ends = [min(rows, (k // block + 1) * block) if dist == REACH else rows for k in range(0, rows, cut)]
        return [(k, k + cut, 0, end) for k, end in zip(range(0, rows, cut), ends)]

    def eights(x):
        return x.reshape(x.shape[0] // 8, 8, x.shape[1])

    def columns(parts, reduce):
        return jnp.concatenate([reduce(t, axis=0, keepdims=True) for t in parts], axis=1)

    def scores(hs, chunks_of, keys, bias):
        tops = [[None] * blocks for _ in hs]
        for k0, k1, q0, q1 in chunks_of:
            for u, h in enumerate(hs):
                s = dot_nt(keys[k0:k1], q_s[h, q0:q1]) * c2 + bias[k0:k1, q0:q1]
                s_s[u, k0:k1, q0:q1] = s
                top = jnp.max(eights(s), axis=0)
                for b in range(q0 // block, q1 // block):
                    part = top[:, b * block - q0 : (b + 1) * block - q0]
                    tops[u][b] = part if tops[u][b] is None else jnp.maximum(tops[u][b], part)
        return [columns(t, jnp.max) for t in tops]

    def weights(hs, chunks_of, ms, dist):
        sums = [[None] * blocks for _ in hs]
        for k0, k1, q0, q1 in chunks_of:
            for u, h in enumerate(hs):
                p = jnp.exp2(s_s[u, k0:k1, q0:q1] - ms[u][:, q0:q1])
                pun[dist, h, k0:k1, q0:q1] = p.astype(BF16)
                low_s[u, k0:k1, q0:q1] = p.astype(BF16)
                part = jnp.sum(eights(p), axis=0)
                for b in range(q0 // block, q1 // block):
                    one = part[:, b * block - q0 : (b + 1) * block - q0]
                    sums[u][b] = one if sums[u][b] is None else sums[u][b] + one
        return [columns(t, jnp.sum) for t in sums]

    def back_chunks(hs, chunks_of, dist, values, dk_sum, dv_sum):
        factors = [f_s[dist, h] for h in hs]
        deltas = [delta_s[h] for h in hs]
        for k0, k1, q0, q1 in chunks_of:
            lows, dss = [], []
            for u, h in enumerate(hs):
                p = pun[dist, h, k0:k1, q0:q1].astype(F32) * factors[u][:, q0:q1]
                dp = dot_nt(values[k0:k1], g_s[h, q0:q1])
                ds = (p * (dp - deltas[u][:, q0:q1])).astype(BF16)
                ds_s[u, k0:k1, q0:q1] = ds
                lows.append(p.astype(BF16))
                dss.append(ds)
            gs = jnp.concatenate([g_s[h, q0:q1] for h in hs], axis=0)
            qs = jnp.concatenate([q_s[h, q0:q1] for h in hs], axis=0)
            dv_sum[k0:k1] += dot(jnp.concatenate(lows, axis=1), gs)
            dk_sum[k0:k1] += dot(jnp.concatenate(dss, axis=1), qs)

    def local_dot(left, right):
        return [dot(left[:, : (b + 1) * block], right[: (b + 1) * block, b * block : (b + 1) * block]) for b in range(blocks)]

    def far_dot(dist, left, right):
        first = block if dist == REACH else 0
        return [dot(left[:, b * first :], right[b * first :, b * block : (b + 1) * block]) for b in range(blocks)]

    def slot_of(dist):
        return pl.ds((REACH - dist) * rows, rows)

    @pl.loop(0, heads, step=GROUP)
    def _(first):
        hs = [first + u for u in range(GROUP)]
        for h in hs:
            for copy in fetch(h):
                copy.wait()
        ms = scores(hs, local_chunks(), k_ref, bias0)
        ls = weights(hs, local_chunks(), ms, 0)
        for u, h in enumerate(hs):
            m_s[0, h] = ms[u]
            l_s[h] = ls[u]
            for b, part in enumerate(local_dot(vt0, low_s.at[u])):
                acc_s[h, :, b * block : (b + 1) * block] = part

    for dist in (2, 1):

        @pl.when(there(-dist))
        def _():
            forward(dist)[0].wait_recv()

        @pl.when(me - dist < 0)
        def _():
            kwin[slot_of(dist)] = jnp.zeros((rows, size), BF16)
            vwin[slot_of(dist)] = jnp.zeros((rows, size), BF16)
            segwin[REACH - dist] = jnp.full((chunks, lanes), -1, jnp.int32)

        seg_far = segwin[REACH - dist].astype(F32)
        for kc in range(chunks):
            col = jnp.transpose(jnp.broadcast_to(seg_far[kc : kc + 1], (lanes, lanes)))
            top = (REACH - dist) * rows + kc * lanes
            for qc in range(chunks):
                value = jnp.where(col == seg_own[qc : qc + 1], 0.0, NEG)
                biasw[top : top + lanes, qc * lanes : (qc + 1) * lanes] = value

    @pl.when(there(-2))
    def _():
        forward(2)[1].wait_recv()

    @pl.when(relays)
    def _():
        relay(0).start()

    @pl.when(there(-2))
    def _():
        forward(2)[2].wait_recv()

    @pl.when(relays)
    def _():
        relay(1).start()

    for dist in (2, 1):
        at = slot_of(dist)
        if dist == 1:

            @pl.when(there(-1))
            def _():
                for copy in forward(1)[1:]:
                    copy.wait_recv()

        ktw[:, at] = jnp.transpose(kwin[at])
        vtw[:, at] = jnp.transpose(vwin[at])

        @pl.loop(0, heads, step=GROUP)
        def _(first):
            hs = [first + u for u in range(GROUP)]
            olds = [m_s[dist_before(dist), h] for h in hs]
            tops = scores(hs, far_chunks(dist), kwin.at[at], biasw.at[at])
            ms = [jnp.maximum(old, top) for old, top in zip(olds, tops)]
            shrink = [jnp.exp2(old - m) for old, m in zip(olds, ms)]
            parts = weights(hs, far_chunks(dist), ms, dist)
            totals = [l_s[h] * a + part for h, a, part in zip(hs, shrink, parts)]
            for u, h in enumerate(hs):
                a, total = shrink[u], totals[u]
                m_s[dist, h] = ms[u]
                sums = []
                for b, part in enumerate(far_dot(dist, vtw.at[:, at], low_s.at[u])):
                    qs = slice(b * block, (b + 1) * block)
                    sums.append(acc_s[h, :, qs] * a[:, qs] + part)
                if dist == REACH:
                    l_s[h] = total
                    for b in range(blocks):
                        acc_s[h, :, b * block : (b + 1) * block] = sums[b]
                else:
                    inv = 1.0 / total
                    f_s[1, h] = inv
                    f_s[2, h] = a * inv
                    f_s[0, h] = jnp.exp2(m_s[0, h] - ms[u]) * inv
                    for b in range(blocks):
                        qs = slice(b * block, (b + 1) * block)
                        out = (sums[b] * inv[:, qs]).astype(BF16).astype(F32)
                        gt = jnp.transpose(g_s[h, qs].astype(F32))
                        delta_s[h, :, qs] = jnp.sum(gt * out, axis=0, keepdims=True)
                        o_s[h, qs] = jnp.transpose(out).astype(BF16)
                    put(h)[0].start()

    for dist in (2, 1):
        at = slot_of(dist)

        @pl.loop(0, heads, step=GROUP)
        def _(first):
            hs = [first + u for u in range(GROUP)]
            back_chunks(hs, far_chunks(dist), dist, vwin.at[at], dkw.at[at], dvw.at[at])
            for u, h in enumerate(hs):
                for b, part in enumerate(far_dot(dist, ktw.at[:, at], ds_s.at[u])):
                    qs = slice(b * block, (b + 1) * block)
                    dqt_s[h, :, qs] = part if dist == REACH else dqt_s[h, :, qs] + part

        outbox[0, dist - 1] = (dkw[at] * scale).astype(BF16)
        outbox[1, dist - 1] = dvw[at].astype(BF16)

        @pl.when(there(-dist))
        def _():
            for copy in back(dist):
                copy.start()

    @pl.loop(0, heads, step=GROUP)
    def _(first):
        hs = [first + u for u in range(GROUP)]
        back_chunks(hs, local_chunks(), 0, v_ref, dk0, dv0)
        for u, h in enumerate(hs):
            for b, part in enumerate(local_dot(kt0, ds_s.at[u])):
                qs = slice(b * block, (b + 1) * block)
                dq_s[h, qs] = jnp.transpose((dqt_s[h, :, qs] + part) * scale).astype(BF16)
            put(h)[1].start()

    dk0[...] = dk0[...] * scale
    for dist in (2, 1):

        @pl.when(there(dist))
        def _():
            for copy in back(dist):
                copy.wait_recv()
            dk0[...] += inbox[0, dist - 1].astype(F32)
            dv0[...] += inbox[1, dist - 1].astype(F32)

    dk_ref[...] = dk0[...].astype(BF16)
    dv_ref[...] = dv0[...].astype(BF16)

    for dist in (1, 2):

        @pl.when(there(dist))
        def _():
            forward(dist)[0].wait_send()

        @pl.when(direct if dist == 1 else there(dist))
        def _():
            for copy in forward(dist)[1:]:
                copy.wait_send()

        @pl.when(there(-dist))
        def _():
            for copy in back(dist):
                copy.wait_send()

    @pl.when(relays)
    def _():
        for i in range(2):
            relay(i).wait_send()

    @pl.loop(0, heads)
    def _(h):
        for copy in put(h):
            copy.wait()


def on_device(n, queries, keys, values, grad_out, segments):
    rows, width = queries.shape
    size = keys.shape[1]
    heads = width // size
    block = rows // 2
    lanes = 128
    far = REACH * rows
    vmem = pl.BlockSpec(memory_space=pltpu.VMEM)
    hbm = pl.BlockSpec(memory_space=pl.ANY)
    far_in = pl.BlockSpec(memory_space=pltpu.HBM)
    wide = jax.ShapeDtypeStruct((rows, width), BF16)
    thin = jax.ShapeDtypeStruct((rows, size), BF16)
    stack = pltpu.VMEM((heads, rows, size), BF16)
    row = pltpu.VMEM((heads, 1, rows), F32)
    rows3 = pltpu.VMEM((REACH + 1, heads, 1, rows), F32)
    tall = pltpu.VMEM((heads, size, rows), F32)
    dma = pltpu.SemaphoreType.DMA
    return pl.pallas_call(
        functools.partial(kernel, n, heads, rows, size, block),
        out_shape=(wide, wide, thin, thin),
        in_specs=[vmem, vmem, vmem, far_in, far_in],
        out_specs=(hbm, hbm, vmem, vmem),
        scratch_shapes=[
            stack, stack, stack, stack,
            pltpu.VMEM((far, size), BF16), pltpu.VMEM((far, size), BF16),
            pltpu.VMEM((REACH, rows // lanes, lanes), jnp.int32),
            pltpu.VMEM((size, far), BF16), pltpu.VMEM((size, far), BF16),
            pltpu.VMEM((size, rows), BF16), pltpu.VMEM((size, rows), BF16),
            pltpu.VMEM((rows, rows), F32), pltpu.VMEM((far, rows), F32),
            pltpu.VMEM((REACH + 1, heads, rows, rows), BF16),
            rows3, row, tall, rows3, row, tall,
            pltpu.VMEM((far, size), F32), pltpu.VMEM((far, size), F32),
            pltpu.VMEM((rows, size), F32), pltpu.VMEM((rows, size), F32),
            pltpu.VMEM((2, REACH, rows, size), BF16), pltpu.VMEM((2, REACH, rows, size), BF16),
            pltpu.VMEM((GROUP, rows, rows), F32),
            pltpu.VMEM((GROUP, rows, rows), BF16), pltpu.VMEM((GROUP, rows, rows), BF16),
            dma((2, heads)), dma((2, heads)),
            dma((3, REACH)), dma((3, REACH)), dma((2,)), dma((2, REACH)), dma((2, REACH)),
        ],
        compiler_params=pltpu.CompilerParams(
            collective_id=0, has_side_effects=True,
            vmem_limit_bytes=VMEM_MIB * 1024 * 1024,
        ),
    )(keys, values, segments.reshape(rows // lanes, lanes), queries, grad_out)


def solution(mesh):
    placed = (P("cp", "grp"), P("cp", "grp"), P("cp", "grp"), P("cp", "grp"), P("cp"))
    return jax.shard_map(
        functools.partial(on_device, mesh.shape["cp"]),
        mesh=mesh,
        in_specs=placed,
        out_specs=(P("cp", "grp"), P("cp", "grp"), P("cp", "grp"), P("cp", "grp")),
        check_vma=False,
    )
```
